32 devices in a mesh: wide: 8 (over z, y), narrow: 4 (over x, core).
Axes of the slice: x: 2, y: 2, z: 4, core: 2. Of those that a mesh axis runs over, the one named last changes fastest.
Arguments:
- hidden_in: bfloat16 [4096, 768], P(('wide', 'narrow')), may hold values from -6 to 6
- frozen_weights: bfloat16 [2, 7087872], P(None, ('wide', 'narrow'))
- adapter_factors: bfloat16 [2, 2, 12, 6912], P(None, None, None, ('wide', 'narrow'))
- strengths: float32 [2, 6, 12], replicated, may hold values from 0.3 to 1.5
- relative: bfloat16 [393216], P(('wide', 'narrow')), may hold values from -6 to 6
- segment_ids: int32 [4096], P(('wide', 'narrow')), may hold values from 0 to 127, as said below
- row_lengths: int32 [32], P(('wide', 'narrow')), may hold values from 1 to 128, as said below
- cotangent: float32 [4096, 768], P(('wide', 'narrow')), may hold values from -6 to 6
Outputs:
- layer_output: float32 [4096, 768], P(('wide', 'narrow'))
- input_grad: float32 [4096, 768], P(('wide', 'narrow'))
- factor_grads: float32 [2, 2, 12, 6912], P(None, None, None, ('wide', 'narrow'))
- strength_grads: float32 [2, 6, 12], replicated
The draws below stay inside these ranges and needn't reach their ends.
Inputs may be any that keep to these rules, and one draw needn't show every extreme that they name: `segment_ids`: within each packed row the ids start at 0, never fall, and each id marks one contiguous document; some row is made of one-token documents, so its ids run up to 127. `row_lengths`: some packed row of the first device is one document filling all 128 slots.
All inputs are finite; a program needn't handle non-finite values.
Results may differ from the reference program's by a relative error of at most 0.022.
Values may be sent and summed in bfloat16 or wider, within the bound.
No kernel may reach another device: no remote copies, remote signals or barrier semaphores. Data moves between devices by JAX's collectives and lax.ppermute only.
A program may use at most 384 MiB of HBM per device.

```python
import math
import jax
import jax.numpy as jnp
import numpy as np
from jax import lax

D = 768
FF = 3072
HEADS = 12
HEAD_DIM = 64
SPAN = 256
RANK = 12
LAYERS = 2
ROW_LEN = 128
ROWS_DEV = 1
ROWS = 32
TOKENS = 4096


def packing(key):
    base = jax.random.fold_in(key, 11)
    first, second, third = jax.random.split(base, 3)
    places = jnp.arange(ROW_LEN, dtype=jnp.int32)
    row_number = jnp.arange(ROWS)
    last_row = row_number == ROWS - 1
    starts = (jax.random.randint(first, (ROWS, ROW_LEN), 0, 24) == 0) | (places[None, :] == 0)
    starts = starts | last_row[:, None]
    single = ((jax.random.randint(second, (ROWS,), 0, 8) == 0) | (row_number < ROWS_DEV)) & jnp.logical_not(last_row)
    starts = jnp.where(single[:, None], places[None, :] == 0, starts)
    segments = jnp.cumsum(starts.astype(jnp.int32), axis=1) - 1
    partial_lengths = jax.random.randint(third, (ROWS,), ROW_LEN // 4, ROW_LEN + 1)
    lengths = jnp.where(single, ROW_LEN, partial_lengths)
    return (segments.reshape(ROWS * ROW_LEN).astype(jnp.int32), lengths.astype(jnp.int32))


def draw_segment_ids(key, part):
    return packing(key)[0]


def draw_row_lengths(key, part):
    return packing(key)[1]


def draw_frozen_weights(key, part):
    total = 4 * D * D + 2 * D * FF + 9 * D + FF
    spot = jnp.arange(total)
    noise = jax.random.normal(jax.random.fold_in(key, 3), (LAYERS, total), jnp.float32)
    square = D * D
    inner_end = 4 * square + D * FF
    matrix_end = inner_end + FF * D
    gains_one = matrix_end + 5 * D + FF
    gains_two = gains_one + 2 * D
    scale = jnp.where(spot < 3 * square, D ** (-0.5), jnp.where(spot < 4 * square, 3.0 * D ** (-0.5), jnp.where(spot < inner_end, D ** (-0.5), jnp.where(spot < matrix_end, 1.5 * FF ** (-0.5), 0.1))))
    is_gain = (spot >= gains_one) & (spot < gains_one + D) | (spot >= gains_two) & (spot < gains_two + D)
    return jnp.where(is_gain[None, :], 1.0 + 0.1 * noise, noise * scale[None, :]).astype(jnp.bfloat16)


def draw_adapter_factors(key, part):
    columns = 5 * D + FF
    noise = jax.random.normal(jax.random.fold_in(key, 5), (LAYERS, 2, RANK, columns), jnp.float32)
    column = jnp.arange(columns)
    down_scale = jnp.where(column < 5 * D, D ** (-0.5), FF ** (-0.5))
    which = jnp.arange(2)[:, None, None]
    scale = jnp.where(which == 0, down_scale[None, None, :], 0.3)
    return (noise * scale[None]).astype(jnp.bfloat16)


def level_of(rng, shape, cuts, smallest, largest):
    level, own = 1.0, jax.random.fold_in(rng, 6)
    for position, parts in cuts:
        draws = jnp.exp(jax.random.uniform(jax.random.fold_in(own, position), (parts,), jnp.float32, smallest / len(cuts), largest / len(cuts)))
        level = level * jnp.repeat(draws, shape[position] // parts).reshape([-1 if axis == position else 1 for axis in range(len(shape))])
    return level


def normal_values(stream_key, shape, scale, bound, cuts=(), kind=jnp.bfloat16):
    factor_of = level_of(stream_key, shape, cuts, -0.22, 0.18) if cuts else 1.0
    drawn = jax.random.normal(stream_key, shape, jnp.float32) * scale * factor_of
    return jnp.minimum(jnp.maximum(drawn, -bound), bound).astype(kind)


def setup_inputs(seed: int = 0) -> dict:
    streams_of = jax.random.split(jax.random.key(seed), 9)
    hidden_in = normal_values(streams_of[0], (TOKENS, D), 1.0, 6.0, ((0, 32),))
    frozen_weights = draw_frozen_weights(jax.random.fold_in(streams_of[8], 71), 0)
    adapter_factors = draw_adapter_factors(jax.random.fold_in(streams_of[8], 71), 0)
    strengths = jnp.clip(jax.random.uniform(streams_of[3], (LAYERS, 6, RANK), jnp.float32, 0.3, 1.5), 0.3, 1.5)
    relative = normal_values(streams_of[4], (2 * SPAN * D,), 1.0, 6.0, ((0, 32),))
    segment_ids = draw_segment_ids(jax.random.fold_in(streams_of[8], 71), 0)
    row_lengths = draw_row_lengths(jax.random.fold_in(streams_of[8], 71), 0)
    cotangent = normal_values(streams_of[7], (TOKENS, D), 1.0, 6.0, ((0, 32),), jnp.float32)
    return dict(hidden_in=hidden_in, frozen_weights=frozen_weights, adapter_factors=adapter_factors, strengths=strengths, relative=relative, segment_ids=segment_ids, row_lengths=row_lengths, cotangent=cotangent)


highest = lax.Precision.HIGHEST

@jax.custom_vjp
def low(v):
    return lax.optimization_barrier(v.astype(jnp.bfloat16)).astype(jnp.float32)

@jax.custom_vjp
def low_back(v):
    return v

def low_keep(v):
    return (low(v), None)

def low_pass(kept, grad):
    return (grad,)

def back_keep(v):
    return (v, None)

def back_low(kept, grad):
    return (low(grad),)
low.defvjp(low_keep, low_pass)
low_back.defvjp(back_keep, back_low)

def high_dot(left, right):
    return jnp.dot(left, right, precision=highest)

def layer_norm(values, gain, shift):
    center = values - lax.optimization_barrier(jnp.mean(values, axis=-1, keepdims=True))
    spread = lax.optimization_barrier(jnp.mean(center * center, axis=-1, keepdims=True))
    return center * lax.rsqrt(spread + 1e-07) * gain + shift

def bucket_reversed(length):
    middle = SPAN // 2
    ratio_log = math.log((2 * SPAN - 1) / middle)
    entries = []
    for distance in range(length - 1, -length, -1):
        size_abs = abs(distance)
        if size_abs <= middle:
            bucket = distance
        else:
            level = middle + math.ceil(math.log(size_abs / middle) / ratio_log * (middle - 1))
            bucket = level if distance > 0 else -level
        entries.append(min(max(bucket + SPAN, 0), 2 * SPAN - 1))
    return np.array(entries, dtype=np.int32)

def shear_rows(places):
    leading = places.shape[:-2]
    length = places.shape[-2]
    columns = places.shape[-1]
    padded = jnp.pad(places, [(0, 0)] * len(leading) + [(0, 0), (0, 1)])
    flattened = padded.reshape(leading + (length * (columns + 1),))
    trimmed = flattened[..., length - 1:length - 1 + length * columns]
    return trimmed.reshape(leading + (length, columns))[..., :length]

def split_weights(packed, factors):
    square = D * D
    inner_end = 4 * square + D * FF
    matrix_end = inner_end + FF * D
    weights = {}
    for number, entry_name in enumerate(('query', 'key', 'value', 'output')):
        weights[entry_name] = packed[number * square:(number + 1) * square].reshape(D, D)
    weights['inner'] = packed[4 * square:inner_end].reshape(D, FF)
    weights['outer'] = packed[inner_end:matrix_end].reshape(FF, D)
    offsets = [0, D, 2 * D, 3 * D, 4 * D, 4 * D + FF, 5 * D + FF, 6 * D + FF, 7 * D + FF, 8 * D + FF]
    extents = [D, D, D, D, FF, D, D, D, D, D]
    labels = ('query_bias', 'key_bias', 'value_bias', 'output_bias', 'inner_bias', 'outer_bias', 'gain_first', 'shift_first', 'gain_second', 'shift_second')
    for offset, extent, entry_name in zip(offsets, extents, labels):
        weights[entry_name] = packed[matrix_end + offset:matrix_end + offset + extent].astype(jnp.float32)
    down_offsets = [0, D, 2 * D, 3 * D, 4 * D, 5 * D]
    down_extents = [D, D, D, D, D, FF]
    up_offsets = [0, D, 2 * D, 3 * D, 4 * D, 4 * D + FF]
    up_extents = [D, D, D, D, FF, D]
    down_maps = [factors[0][:, o:o + e] for o, e in zip(down_offsets, down_extents)]
    up_maps = [factors[1][:, o:o + e] for o, e in zip(up_offsets, up_extents)]
    return (weights, down_maps, up_maps)

def build_masks(segments, lengths):
    places = jnp.arange(segments.shape[1], dtype=jnp.int32)
    valid = places[None, :] < lengths[:, None]
    allowed = (segments[:, :, None] == segments[:, None, :]) & valid[:, :, None] & valid[:, None, :]
    return (allowed, valid.astype(jnp.float32))

def attention_core(query, keyed, values, rel_keys, rel_queries, allowed, valid):
    groups, length, width = query.shape
    order_back = jnp.asarray(bucket_reversed(length))
    chooser = (order_back[None, :] == jnp.arange(2 * SPAN, dtype=jnp.int32)[:, None]).astype(jnp.float32)
    keys_far = jnp.dot(chooser.T, rel_keys, precision=highest).reshape(2 * length - 1, HEADS, HEAD_DIM)
    queries_far = jnp.dot(chooser.T, rel_queries, precision=highest).reshape(2 * length - 1, HEADS, HEAD_DIM)
    query_heads = query.reshape(groups, length, HEADS, HEAD_DIM)
    key_heads = keyed.reshape(groups, length, HEADS, HEAD_DIM)
    value_heads = values.reshape(groups, length, HEADS, HEAD_DIM)
    content = jnp.einsum('gihd,gjhd->ghij', query_heads, key_heads, precision=highest)
    query_place = jnp.einsum('gihd,rhd->ghir', query_heads, keys_far, precision=highest)
    key_place = jnp.einsum('gjhd,rhd->ghjr', key_heads, queries_far, precision=highest)
    to_place = shear_rows(query_place)
    from_place = jnp.swapaxes(shear_rows(key_place), 2, 3)
    scores = (content + to_place + from_place) * (1.0 / math.sqrt(3 * HEAD_DIM))
    permit = allowed[:, None, :, :]
    masked = jnp.where(permit, scores, -1e+30)
    highest_score = lax.optimization_barrier(jnp.max(masked, axis=3, keepdims=True))
    weights_raw = jnp.where(permit, jnp.exp(masked - highest_score), 0.0)
    totals = lax.optimization_barrier(jnp.sum(weights_raw, axis=3, keepdims=True)) + (1.0 - valid[:, None, :, None])
    probs = weights_raw / totals
    context = jnp.einsum('ghij,gjhd->gihd', probs, value_heads, precision=highest)
    return context.reshape(groups, length, width)

def forward_layer(state_rows, packed, factors, scales, table, allowed, valid):
    weights, down_maps, up_maps = split_weights(packed, factors)

    def adapted(inputs, number, entry_name):
        reduced = high_dot(inputs, down_maps[number].T) * scales[number]
        return high_dot(inputs, weights[entry_name]) + weights[entry_name + '_bias'] + high_dot(reduced, up_maps[number])
    inputs_low = low(state_rows)
    query = low_back(adapted(inputs_low, 0, 'query'))
    keyed = low_back(adapted(inputs_low, 1, 'key'))
    values = low_back(adapted(inputs_low, 2, 'value'))
    rel_keys = adapted(table, 1, 'key')
    rel_queries = adapted(table, 0, 'query')
    context = attention_core(query, keyed, values, rel_keys, rel_queries, allowed, valid)
    first = layer_norm(state_rows + low_back(adapted(low(context), 3, 'output')), weights['gain_first'], weights['shift_first'])
    hidden = low_back(adapted(low(first), 4, 'inner'))
    active = jax.nn.gelu(hidden, approximate=False)
    second = first + low_back(adapted(low(active), 5, 'outer'))
    return layer_norm(second, weights['gain_second'], weights['shift_second'])

def reference(hidden_in, frozen_weights, adapter_factors, strengths, relative, segment_ids, row_lengths, cotangent):
    frozen = frozen_weights.astype(jnp.float32)
    factors = adapter_factors.astype(jnp.float32)
    table = layer_norm(relative.astype(jnp.float32).reshape(2 * SPAN, D), 1.0, 0.0)
    group_rows = math.gcd(ROWS, max(1, 4096 // ROW_LEN))
    group_count = ROWS // group_rows
    states = hidden_in.astype(jnp.float32).reshape(group_count, group_rows, ROW_LEN, D)
    segments = segment_ids.reshape(group_count, group_rows, ROW_LEN)
    lengths = row_lengths.reshape(group_count, group_rows)
    grads_in = cotangent.reshape(group_count, group_rows, ROW_LEN, D)

    def scan_step(running, entries):
        state_rows, segment_rows, length_rows, grad_rows = entries
        allowed, valid = build_masks(segment_rows, length_rows)

        def forward(inputs, factor_all, scale_all):
            current = inputs
            for layer_index in range(LAYERS):
                current = forward_layer(current, frozen[layer_index], factor_all[layer_index], scale_all[layer_index], table, allowed, valid)
            return current
        output, pullback = jax.vjp(forward, state_rows, factors, strengths)
        grad_state, grad_factors, grad_scales = pullback(grad_rows)
        return ((running[0] + grad_factors, running[1] + grad_scales), (output, grad_state))
    starting = (jnp.zeros(factors.shape, jnp.float32), jnp.zeros(strengths.shape, jnp.float32))
    totals, (outputs, grads) = lax.scan(scan_step, starting, (states, segments, lengths, grads_in))
    return (outputs.reshape(TOKENS, D), grads.reshape(TOKENS, D), totals[0], totals[1])
```

```python
import functools
import math

import jax
import jax.numpy as jnp
import numpy as np
from jax import lax
from jax.experimental import pallas as pl
from jax.experimental.pallas import tpu as pltpu
from jax.sharding import PartitionSpec as P

D = 768
FF = 3072
HEADS = 12
HEAD_DIM = 64
SPAN = 256
RANK = 12
LAYERS = 2
ROW_LEN = 128
PAIRS = HEADS // 2
MAT_ROWS = 12 * D
TAIL_ROWS = 13
TAIL = TAIL_ROWS * D
COLS = 5 * D + FF
RP = 16
UNIT = 96
SCALE = 1.0 / math.sqrt(3 * HEAD_DIM)
BOTH = ("wide", "narrow")
f32 = jnp.float32
bf16 = jnp.bfloat16


def nn(a, b):
    return lax.dot_general(a, b, (((1,), (0,)), ((), ())), preferred_element_type=f32)


def nt(a, b):
    return lax.dot_general(a, b, (((1,), (1,)), ((), ())), preferred_element_type=f32)


def tn(a, b):
    return lax.dot_general(a, b, (((0,), (0,)), ((), ())), preferred_element_type=f32)


def fetch_weights(arrays, cut, places, w, sems, late_first):
    parts = arrays
    if not cut:
        for u in range(MAT_ROWS // UNIT):
            mat = u // 8
            if 4 <= mat < 8:
                for k in range(4):
                    dst = 4 * D + k * D + (u - 32) * 24
                    pltpu.make_async_copy(
                        parts[0].at[pl.ds(u * UNIT + k * 24, 24)], w.at[pl.ds(dst, 24)], sems.at[4]
                    ).start()
            elif u % 8 == 0:
                pltpu.make_async_copy(
                    parts[0].at[pl.ds(mat * D, D)], w.at[pl.ds(mat * D, D)], sems.at[mat]
                ).start()
        return
    rows = MAT_ROWS // len(cut)
    parts = []
    for number, start in cut:
        parts.append(arrays[number].at[pl.ds(start, rows)])
    units = rows // UNIT
    border = 4 * D // rows + 1

    def copy_block(part, place):
        def copy_unit(j, carry):
            u = place * units + j
            at = pl.multiple_of(j * UNIT, 8)
            inner = (u >= 32) & (u < 64)

            @pl.when(inner)
            def _():
                for k in range(4):
                    dst = pl.multiple_of(4 * D + k * D + (u - 32) * 24, 8)
                    pltpu.make_async_copy(
                        part.at[pl.ds(pl.multiple_of(at + k * 24, 8), 24)],
                        w.at[pl.ds(dst, 24)],
                        sems.at[4],
                    ).start()

            @pl.when(jnp.logical_not(inner))
            def _():
                pltpu.make_async_copy(
                    part.at[pl.ds(at, UNIT)],
                    w.at[pl.ds(pl.multiple_of(u * UNIT, 8), UNIT)],
                    sems.at[u // 8],
                ).start()

            return carry

        lax.fori_loop(0, units, copy_unit, 0)

    for late in (late_first, not late_first):
        for i, part in enumerate(parts):
            place = places[i]

            @pl.when((place >= border) == late)
            def _():
                copy_block(part, place)


def wait_rows(w, sems, mat, count=1):
    pltpu.make_async_copy(
        w.at[pl.ds(0, count * D)], w.at[pl.ds(0, count * D)], sems.at[mat]
    ).wait()


def norm_parts(z):
    center = z - jnp.mean(z, axis=1, keepdims=True)
    rinv = lax.rsqrt(jnp.mean(center * center, axis=1, keepdims=True) + 1e-07)
    return center * rinv, rinv


def norm_grad(upstream, gain, xhat, rinv):
    gy = upstream * gain
    return rinv * (
        gy
        - jnp.mean(gy, axis=1, keepdims=True)
        - xhat * jnp.mean(gy * xhat, axis=1, keepdims=True)
    )


def split_pair(block):
    low = lax.broadcasted_iota(jnp.int32, block.shape, 1) < HEAD_DIM
    zero = jnp.zeros_like(block)
    return jnp.concatenate([jnp.where(low, block, zero), jnp.where(low, zero, block)], axis=0)


def halves_side(block):
    half = block.shape[0] // 2
    return jnp.concatenate([block[:half], block[half:]], axis=1)


def skew(block):
    return pltpu.roll(block, 2 * ROW_LEN - ROW_LEN + 1, 1, stride=1, stride_axis=0)[:, :ROW_LEN]


def unskew(block):
    wide = jnp.concatenate([block, jnp.zeros_like(block)], axis=1)
    return pltpu.roll(wide, 0, 1, stride=1, stride_axis=0)


def forward_kernel(
    count, cut, x_ref, places, bias_ref, pt_ref, q_ref, l_ref, tab_ref, segc_ref, segr_ref, *refs,
):
    parts, refs = refs[:count], refs[count:]
    y_ref, qkv_ref, rel_ref, p_ref, ctx_ref, xh1_ref, gp_ref, ab_ref, xh2_ref = refs[:9]
    rinv_ref, t_ref, w, rel, sems = refs[9:]
    fetch_weights(parts, cut, places, w, sems, False)
    x = x_ref[...].astype(f32)
    xb = x.astype(bf16)

    def bias(row):
        return bias_ref[row : row + 1, :]

    def scale(m):
        return l_ref[m : m + 1, :RP]

    rows = jnp.concatenate([xb, tab_ref[...]], axis=0)
    t_ref[...] = jnp.zeros_like(t_ref)
    for m in range(3):
        inputs = rows if m < 2 else xb
        t = nt(inputs, pt_ref[:, m * D : (m + 1) * D])
        t_ref[:, m * RP : (m + 1) * RP] = t[:ROW_LEN]
        low = (t * scale(m)).astype(bf16)
        wait_rows(w, sems, m)
        out = nn(inputs, w[m * D : (m + 1) * D, :]) + nn(low, q_ref[:, m * D : (m + 1) * D])
        out = (out + bias(m)).astype(bf16)
        qkv_ref[m] = out[:ROW_LEN]
        if m < 2:
            rel[m] = out[ROW_LEN:]
    allowed = segc_ref[...] == segr_ref[...]
    allowed = jnp.concatenate([allowed, allowed], axis=0)
    turn_row = lax.broadcasted_iota(jnp.int32, (2 * ROW_LEN, 2 * ROW_LEN), 0)
    turn_col = lax.broadcasted_iota(jnp.int32, (2 * ROW_LEN, 2 * ROW_LEN), 1)
    turn = (turn_row + turn_col == 2 * ROW_LEN - 2).astype(f32).astype(bf16)
    for m in range(2):
        rel_ref[m] = nn(turn, rel[m]).astype(bf16)

    def pair_step(pp, carry):
        lanes = pl.ds(pl.multiple_of(pp * 128, 128), 128)
        kp = qkv_ref[1, :, lanes]
        q2 = split_pair(qkv_ref[0, :, lanes])
        k2 = split_pair(kp)
        content = nt(q2, kp)
        to_rel = nt(q2, rel[1, :, lanes])
        from_rel = nt(k2, rel[0, :, lanes])
        to_place = jnp.concatenate([skew(to_rel[:ROW_LEN]), skew(to_rel[ROW_LEN:])], axis=0)
        from_place = jnp.concatenate(
            [skew(from_rel[:ROW_LEN]).T, skew(from_rel[ROW_LEN:]).T], axis=0
        )
        scores = (content + to_place + from_place) * SCALE
        masked = jnp.where(allowed, scores, -1e30)
        top = jnp.max(masked, axis=1, keepdims=True)
        raw = jnp.where(allowed, jnp.exp(masked - top), 0.0)
        total = jnp.sum(raw, axis=1, keepdims=True)
        probs = (raw / jnp.where(total > 0.0, total, 1.0)).astype(bf16)
        p_ref[pp] = probs
        ctx = nn(halves_side(probs), split_pair(qkv_ref[2, :, lanes]))
        ctx_ref[:, lanes] = ctx.astype(bf16)
        return carry

    lax.fori_loop(0, PAIRS, pair_step, 0)

    ctx = ctx_ref[...]
    t = nt(ctx, pt_ref[:, 3 * D : 4 * D])
    t_ref[:, 3 * RP : 4 * RP] = t
    wait_rows(w, sems, 3)
    out = nn(ctx, w[3 * D : 4 * D, :]) + nn((t * scale(3)).astype(bf16), q_ref[:, 3 * D : 4 * D])
    xhat, rinv = norm_parts(x + out + bias(3))
    xh1_ref[...] = xhat
    rinv_ref[:, 0:128] = jnp.broadcast_to(rinv, (ROW_LEN, 128))
    first = xhat * bias(9) + bias(10)
    first_low = first.astype(bf16)
    t = nt(first_low, pt_ref[:, 4 * D : 5 * D])
    t_ref[:, 4 * RP : 5 * RP] = t
    t_in = (t * scale(4)).astype(bf16)
    wait_rows(w, sems, 4, 4)

    def ff_step(k, carry):
        acc, t_acc = carry
        at = pl.multiple_of(k * D, D)
        u = nn(first_low, w[pl.ds(4 * D + at, D), :]) + nn(t_in, q_ref[:, pl.ds(4 * D + at, D)])
        u = u + bias_ref[pl.ds(4 + k, 1), :]
        cdf = 0.5 * (1.0 + lax.erf(u * math.sqrt(0.5)))
        gp_ref[k] = (cdf + u * jnp.exp(-0.5 * u * u) * (1.0 / math.sqrt(2 * math.pi))).astype(bf16)
        act = (u * cdf).astype(bf16)
        ab_ref[k] = act
        wait_rows(w, sems, 8 + k)
        acc = acc + nn(act, w[pl.ds(8 * D + at, D), :])
        t_acc = t_acc + nt(act, pt_ref[:, pl.ds(5 * D + at, D)])
        return acc, t_acc

    acc, t = lax.fori_loop(
        0, 4, ff_step, (jnp.zeros((ROW_LEN, D), f32), jnp.zeros((ROW_LEN, RP), f32))
    )
    t_ref[:, 5 * RP : 6 * RP] = t
    out = acc + nn((t * scale(5)).astype(bf16), q_ref[:, 8 * D : 9 * D])
    xhat, rinv = norm_parts(first + out + bias(8))
    xh2_ref[...] = xhat
    rinv_ref[:, 128:256] = jnp.broadcast_to(rinv, (ROW_LEN, 128))
    y_ref[...] = xhat * bias(11) + bias(12)


def backward_kernel(
    count, cut, g_ref, x_ref, places, bias_ref, pt_ref, q_ref, l_ref, lt_ref, tab_ref,
    qkv_ref, rel_ref, p_ref, ctx_ref, xh1_ref, gp_ref, ab_ref, xh2_ref, rinv_ref, t_ref,
    *refs,
):
    parts, refs = refs[:count], refs[count:]
    dx_ref, dpt_ref, dq_ref, dl_ref, w, dctx_s, dqkv, drel, sems = refs
    fetch_weights(parts, cut, places, w, sems, True)
    dl_ref[...] = jnp.zeros_like(dl_ref)

    def bias(row):
        return bias_ref[row : row + 1, :]

    def scale(m):
        return l_ref[m : m + 1, :RP]

    def t_low(m):
        return t_ref[:, m * RP : (m + 1) * RP].astype(bf16)

    def put_up(m, cols, raw):
        dq_ref[:, cols] = raw * lt_ref[:, m : m + 1]
        part = jnp.sum(raw * q_ref[:, cols].astype(f32), axis=1, keepdims=True)
        dl_ref[:, m : m + 1] = dl_ref[:, m : m + 1] + part

    dz2 = norm_grad(g_ref[...], bias(11), xh2_ref[...], rinv_ref[:, 128:129])
    h = dz2.astype(bf16)
    e_out = (nt(h, q_ref[:, 8 * D : 9 * D]) * scale(5)).astype(bf16)
    put_up(5, slice(8 * D, 9 * D), tn(t_low(5), h))
    t_in = t_low(4)
    wait_rows(w, sems, 4, 4)

    def ff_step(k, carry):
        acc, e_acc = carry
        at = pl.multiple_of(k * D, D)
        wait_rows(w, sems, 8 + k)
        pcols = pl.ds(5 * D + at, D)
        qcols = pl.ds(4 * D + at, D)
        dab = nt(h, w[pl.ds(8 * D + at, D), :]) + nn(e_out, pt_ref[:, pcols])
        du = (gp_ref[k].astype(f32) * dab).astype(bf16)
        acc = acc + nt(du, w[pl.ds(4 * D + at, D), :])
        e_acc = e_acc + nt(du, q_ref[:, qcols])
        dpt_ref[:, pcols] = tn(e_out, ab_ref[k])
        put_up(4, qcols, tn(t_in, du))
        return acc, e_acc

    acc, e_in = lax.fori_loop(
        0, 4, ff_step, (jnp.zeros((ROW_LEN, D), f32), jnp.zeros((ROW_LEN, RP), f32))
    )
    e_in = (e_in * scale(4)).astype(bf16)
    dfirst = dz2 + acc + nn(e_in, pt_ref[:, 4 * D : 5 * D])
    first_low = (xh1_ref[...] * bias(9) + bias(10)).astype(bf16)
    dpt_ref[:, 4 * D : 5 * D] = tn(e_in, first_low)
    dz1 = norm_grad(dfirst, bias(9), xh1_ref[...], rinv_ref[:, 0:1])
    h = dz1.astype(bf16)
    e_o = (nt(h, q_ref[:, 3 * D : 4 * D]) * scale(3)).astype(bf16)
    put_up(3, slice(3 * D, 4 * D), tn(t_low(3), h))
    dpt_ref[:, 3 * D : 4 * D] = tn(e_o, ctx_ref[...])
    wait_rows(w, sems, 3)
    dctx_s[...] = (nt(h, w[3 * D : 4 * D, :]) + nn(e_o, pt_ref[:, 3 * D : 4 * D])).astype(bf16)

    turn_row = lax.broadcasted_iota(jnp.int32, (ROW_LEN, ROW_LEN), 0)
    turn_col = lax.broadcasted_iota(jnp.int32, (ROW_LEN, ROW_LEN), 1)
    turn = (turn_row + turn_col == ROW_LEN - 1).astype(f32).astype(bf16)

    def pair_step(pp, carry):
        lanes = pl.ds(pl.multiple_of(pp * 128, 128), 128)
        q2 = split_pair(qkv_ref[0, :, lanes])
        k2 = split_pair(qkv_ref[1, :, lanes])
        d2 = split_pair(dctx_s[:, lanes])
        probs = p_ref[pp]
        p = probs.astype(f32)
        dp = nt(d2, qkv_ref[2, :, lanes])
        ds = p * (dp - jnp.sum(p * dp, axis=1, keepdims=True)) * SCALE
        ds_t = jnp.concatenate([ds[:ROW_LEN].T, ds[ROW_LEN:].T], axis=0).astype(bf16)
        ds = ds.astype(bf16)
        back = nn(ds, turn)
        back_t = nn(ds_t, turn)
        far = jnp.concatenate([unskew(back[:ROW_LEN]), unskew(back[ROW_LEN:])], axis=0)
        far = far.astype(bf16)
        far_t = jnp.concatenate([unskew(back_t[:ROW_LEN]), unskew(back_t[ROW_LEN:])], axis=0)
        far_t = far_t.astype(bf16)
        kr2 = split_pair(rel_ref[1, :, lanes])
        qr2 = split_pair(rel_ref[0, :, lanes])
        dqkv[0, :, lanes] = (nn(halves_side(ds), k2) + nn(halves_side(far), kr2)).astype(bf16)
        dqkv[1, :, lanes] = (nn(halves_side(ds_t), q2) + nn(halves_side(far_t), qr2)).astype(bf16)
        dqkv[2, :, lanes] = tn(probs, d2).astype(bf16)
        drel[1, :, lanes] = tn(far, q2).astype(bf16)
        drel[0, :, lanes] = tn(far_t, k2).astype(bf16)
        return carry

    lax.fori_loop(0, PAIRS, pair_step, 0)

    xb = x_ref[...].astype(bf16)
    rows = jnp.concatenate([xb, tab_ref[...]], axis=0)
    dx = dz1
    for m in range(3):
        cols = slice(m * D, (m + 1) * D)
        h = dqkv[m]
        if m < 2:
            h_all = jnp.concatenate([h, drel[m]], axis=0)
            t_tab = nt(tab_ref[...], pt_ref[:, cols])
            t_all = jnp.concatenate([t_ref[:, m * RP : (m + 1) * RP], t_tab], axis=0).astype(bf16)
            inputs = rows
        else:
            h_all, t_all, inputs = h, t_low(m), xb
        e = (nt(h_all, q_ref[:, cols]) * scale(m)).astype(bf16)
        put_up(m, cols, tn(t_all, h_all))
        dpt_ref[:, cols] = tn(e, inputs)
        wait_rows(w, sems, m)
        dx = dx + nt(h, w[cols, :]) + nn(e[:ROW_LEN], pt_ref[:, cols])
    dx_ref[...] = dx


LIMIT = 60 << 20
VM = pl.BlockSpec(memory_space=pltpu.VMEM)
ANY = pl.BlockSpec(memory_space=pl.ANY)
SM = pl.BlockSpec(memory_space=pltpu.SMEM)


def shape(dims, kind):
    return jax.ShapeDtypeStruct(dims, kind)


def run_forward(x, held, places, bias, pt, q, l, tab, segc, segr):
    parts, cut = held
    outs = [
        shape((ROW_LEN, D), f32),
        shape((3, ROW_LEN, D), bf16),
        shape((2, 2 * ROW_LEN, D), bf16),
        shape((PAIRS, 2 * ROW_LEN, ROW_LEN), bf16),
        shape((ROW_LEN, D), bf16),
        shape((ROW_LEN, D), f32),
        shape((4, ROW_LEN, D), bf16),
        shape((4, ROW_LEN, D), bf16),
        shape((ROW_LEN, D), f32),
        shape((ROW_LEN, 256), f32),
        shape((ROW_LEN, 128), f32),
    ]
    return pl.pallas_call(
        functools.partial(forward_kernel, len(parts), cut),
        out_shape=outs,
        in_specs=[VM, SM] + [VM] * 7 + [ANY] * len(parts),
        out_specs=[VM] * len(outs),
        scratch_shapes=[
            pltpu.VMEM((MAT_ROWS, D), bf16),
            pltpu.VMEM((2, 2 * ROW_LEN, D), bf16),
            pltpu.SemaphoreType.DMA((12,)),
        ],
        compiler_params=pltpu.CompilerParams(vmem_limit_bytes=LIMIT),
        cost_estimate=pl.CostEstimate(
            flops=2 * ROW_LEN * MAT_ROWS * D, bytes_accessed=24 << 20, transcendentals=1 << 20
        ),
        name="layer_forward",
    )(x, places, bias, pt, q, l, tab, segc, segr, *parts)


def run_backward(g, x, held, places, bias, pt, q, l, lt, tab, record):
    parts, cut = held
    outs = [
        shape((ROW_LEN, D), f32),
        shape((RP, COLS), f32),
        shape((RP, COLS), f32),
        shape((RP, 128), f32),
    ]
    return pl.pallas_call(
        functools.partial(backward_kernel, len(parts), cut),
        out_shape=outs,
        in_specs=[VM, VM, SM] + [VM] * (6 + len(record)) + [ANY] * len(parts),
        out_specs=[VM] * len(outs),
        scratch_shapes=[
            pltpu.VMEM((MAT_ROWS, D), bf16),
            pltpu.VMEM((ROW_LEN, D), bf16),
            pltpu.VMEM((3, ROW_LEN, D), bf16),
            pltpu.VMEM((2, 2 * ROW_LEN, D), bf16),
            pltpu.SemaphoreType.DMA((12,)),
        ],
        compiler_params=pltpu.CompilerParams(vmem_limit_bytes=LIMIT),
        cost_estimate=pl.CostEstimate(
            flops=4 * ROW_LEN * MAT_ROWS * D, bytes_accessed=24 << 20, transcendentals=1 << 20
        ),
        name="layer_backward",
    )(g, x, places, bias, pt, q, l, lt, tab, *record, *parts)


def align_blocks(frozen, count, place):
    held = frozen.shape[1]
    rows = MAT_ROWS // count
    tail = frozen[:, held - TAIL :]
    before = lax.ppermute(tail, BOTH, [(i, (i + 1) % count) for i in range(count)])
    joined = jnp.concatenate([before, frozen], axis=1)
    start = TAIL - (held - rows * D) * place
    block = lax.dynamic_slice(joined, (0, start), (LAYERS, rows * D))
    return block.reshape(LAYERS, rows, D), tail, before


def unit_order(block, count, place):
    units = MAT_ROWS // count // UNIT
    turn = np.zeros((UNIT, UNIT), np.float32)
    for k in range(4):
        for r in range(24):
            turn[k * 24 + r, 4 * r + k] = 1
    number = units * place + jnp.arange(units)
    inner = (number >= 32) & (number < 64)
    turn = jnp.where(inner[:, None, None], jnp.asarray(turn), jnp.eye(UNIT, dtype=f32)).astype(bf16)
    split = block.reshape(LAYERS, units, UNIT, D)
    return jnp.einsum("uab,lubd->luad", turn, split).astype(bf16).reshape(block.shape)


def unit_order_whole(layer):
    inner = layer[4 * D : 8 * D].reshape(32, 24, 4, D)
    inner = jnp.swapaxes(inner, 1, 2).reshape(4 * D, D)
    return jnp.concatenate([layer[: 4 * D], inner, layer[8 * D :]], axis=0)


ALL = range(32)
TO_CORE = [(d, d ^ 1) for d in ALL]
TO_Z1 = [(d, d ^ 8) for d in ALL]
TO_Z2 = [(d, d ^ 16) for d in ALL]
TO_Z3 = [(d, d ^ 24) for d in ALL]
TO_DIAGONAL = [(d, d ^ 6) for d in ALL]
TO_FIRST = [(d, d ^ (4 if d % 2 else 2)) for d in ALL]
TO_OTHER = [(d, d ^ (2 if d % 2 else 4)) for d in ALL]
Z_ORDER = (0, 16, 8, 24)


def send(value, route):
    return lax.ppermute(value, BOTH, route)


def flip(a, b):
    return a + b - 2 * a * b


def block_move(place, other, along, step):
    swapped = (place % 2 + other) % 2
    first, second = step % 2, step // 2
    move = jnp.where(swapped == 0, 2 * first + 4 * second, 4 * first + 2 * second)
    return (move + along + other).astype(jnp.int32)


def block_places(place):
    number = np.arange(32)
    other, step, along = number // 16, (number // 4) % 4, np.asarray(Z_ORDER)[number % 4]
    return jnp.bitwise_xor(place, block_move(place, other, along, step))


EVENTS = """
S A0 S B0 S o2 S o1
D A0 D B0 D o2 D o1
S o3 S E0 S co0 S co1 S co2
D o3 D E0 D co0 D co1 D co2
S x02 S x01 S A1 S B1 S co3 M -
D x02 D x01 D A1 D B1 D co3
S x03 S E1 S cx00 S cx01 S cx02
D x03 D E1 D cx00 D cx01 D cx02
S cx03 S x12 S x11 D cx03
F -
D x12 D x11
S x13 S cx10 S cx11 S cx12
D x13 D cx10 D cx11 D cx12
S cx13 D cx13
"""
SPARE = 32


class Ordered:
    def __init__(self, own, rows, small, token):
        self.value = {"o0": own}
        self.rows = rows
        self.small = small
        self.token = token
        self.ended = []
        self.fresh = False
        words = EVENTS.split()
        self.before = words[: words.index("F")]
        self.after = words[words.index("F") + 2 :]

    def tie(self, value):
        if not self.ended:
            return value
        value, self.token, *_ = lax.optimization_barrier((value, self.token, *self.ended))
        self.fresh = True
        return value

    def end(self, *values):
        if self.fresh:
            self.ended = []
            self.fresh = False
        self.ended.extend(values)

    def get(self, name):
        value = self.value
        if name not in value:
            value[name] = jnp.concatenate([value[f"{k}{name[1]}"] for k in "ABE"])
        return value[name]

    def source(self, name):
        if name[0] == "c":
            return self.get(name[1:]), TO_CORE
        if name[0] in "AB":
            own = self.value["o0"]
            cut = self.rows + SPARE
            block = own[:cut] if name[1] == "0" else own[cut:]
            return block, TO_Z2 if name[0] == "A" else TO_Z1
        if name[0] == "E":
            return self.get(f"A{name[1]}"), TO_Z1
        base, step = name[:-1], name[-1]
        if step == "3":
            return self.get(base + "2"), TO_FIRST
        return self.get(base + "0"), TO_FIRST if step == "1" else TO_OTHER

    def run(self, words):
        for act, name in zip(words[::2], words[1::2]):
            if act == "M":
                self.end(*self.small)
            elif act == "S":
                value, route = self.source(name)
                self.value[name] = send(self.tie(value), route)
            else:
                self.end(self.get(name))

    def layer(self, i):
        tall = self.rows + (0 if i else SPARE)
        bases = ["o", f"x{i}"]
        names = [f"{lead}{base}{step}" for lead in ("", "c") for step in range(4) for base in bases]
        cut = []
        for lead in ("", "c"):
            for step in range(4):
                cut.append((names.index(f"{lead}o{step}"), i * (self.rows + SPARE)))
                for block in range(3):
                    cut.append((names.index(f"{lead}x{i}{step}"), block * tall))
        return [self.get(name) for name in names], tuple(cut)


NEAR = 17


def unpack_kernel(count, cut, rows, places, *refs):
    parts = refs[:count]
    bias_ref, fac_ref, back_ref, on_ref, spare, near, whole, sem = refs[count:]
    for i, (number, start) in enumerate(cut):
        pltpu.make_async_copy(
            parts[number].at[pl.ds(start + rows, SPARE)], spare.at[places[i]], sem
        ).start()
    pltpu.make_async_copy(spare, spare, sem).wait()
    bias_ref[0] = spare[31, :16].astype(f32)
    bias_ref[1] = spare[0, :16].astype(f32)
    for p in range(NEAR):
        near[16 * p : 16 * p + 16, :] = spare[8 + p, :16].astype(f32)
    raw = near[...]
    center = raw - jnp.mean(raw, axis=1, keepdims=True)
    near[...] = center * lax.rsqrt(jnp.mean(center * center, axis=1, keepdims=True) + 1e-07)
    on_ref[...] = near[1 : 1 + 2 * ROW_LEN, :].astype(bf16)
    row = lax.broadcasted_iota(jnp.int32, (2 * ROW_LEN, 2 * ROW_LEN), 0)
    col = lax.broadcasted_iota(jnp.int32, (2 * ROW_LEN, 2 * ROW_LEN), 1)
    turn = (row + col == 2 * ROW_LEN - 1).astype(f32).astype(bf16)
    back_ref[...] = nn(turn, near[: 2 * ROW_LEN, :].astype(bf16)).astype(bf16)
    cols = COLS // 32
    gap = jnp.zeros((RP - RANK, COLS), bf16)
    for i in range(LAYERS):
        for g in range(3):
            pieces = [
                spare[p, 16:, 256 * g : 256 * g + cols].astype(f32)[8 * i : 8 * i + 8]
                for p in range(32)
            ]
            whole[8 * g : 8 * g + 8, :] = jnp.concatenate(pieces, axis=1)
        for k in range(2):
            fac_ref[2 * i + k, :RANK] = whole[RANK * k : RANK * k + RANK, :].astype(bf16)
            fac_ref[2 * i + k, RANK:] = gap


def unpack(places, held, rows):
    parts, cut = held
    return pl.pallas_call(
        functools.partial(unpack_kernel, len(parts), cut, rows),
        out_shape=[
            shape((LAYERS, 16, D), f32),
            shape((4, RP, COLS), bf16),
            shape((2 * ROW_LEN, D), bf16),
            shape((2 * ROW_LEN, D), bf16),
        ],
        in_specs=[SM] + [ANY] * len(parts),
        out_specs=[VM] * 4,
        scratch_shapes=[
            pltpu.VMEM((32, SPARE, D), bf16),
            pltpu.VMEM((16 * NEAR, D), f32),
            pltpu.VMEM((2 * RANK, COLS), f32),
            pltpu.SemaphoreType.DMA,
        ],
        compiler_params=pltpu.CompilerParams(vmem_limit_bytes=LIMIT),
        name="unpack",
    )(places, *parts)


def gather_all(frozen, factors, relative, count, place, small):
    block, tail, before = align_blocks(frozen, count, place)
    block = unit_order(block, count, place)
    pad = ((0, 16 - TAIL_ROWS), (0, 0))
    slot = jnp.where(
        place == count - 1,
        jnp.pad(tail[0].reshape(TAIL_ROWS, D), pad),
        jnp.where(
            place == 0,
            jnp.pad(before[1].reshape(TAIL_ROWS, D), pad),
            relative.reshape(16, D),
        ),
    )
    cols = COLS // count
    narrow = jnp.pad(factors.reshape(LAYERS, 3, 8, cols), ((0, 0),) * 3 + ((0, 256 - cols),))
    narrow = jnp.swapaxes(narrow, 1, 2).reshape(16, D)
    rows = block.shape[1]
    own = jnp.concatenate([block[0], slot, narrow, block[1]])
    places = block_places(place)
    flow = Ordered(own, rows, [places, *small], place)
    flow.run(flow.before)
    places, *small = flow.small
    bias, fac, tab_back, tab_on = unpack(places, flow.layer(0), rows)
    fac = fac.reshape(LAYERS, 2, RP, COLS)
    return flow, places, bias, fac, tab_back, tab_on, small


def gather_plain(frozen, factors, relative, count, place, small):
    block, tail, _ = align_blocks(frozen, count, place)
    layers = [
        ([unit_order_whole(lax.all_gather(block[i], BOTH, axis=0, tiled=True))], ())
        for i in range(LAYERS)
    ]
    bias = lax.psum(jnp.where(place == count - 1, tail, 0).astype(f32), BOTH)
    bias = bias.reshape(LAYERS, TAIL_ROWS, D)
    bias = jnp.pad(bias, ((0, 0), (0, 16 - TAIL_ROWS), (0, 0)))
    factors = lax.all_gather(factors, BOTH, axis=3, tiled=True)
    factors = jnp.pad(factors, ((0, 0), (0, 0), (0, RP - RANK), (0, 0)))
    table = lax.all_gather(relative, BOTH, axis=0, tiled=True).reshape(2 * SPAN, D).astype(f32)
    center = table - jnp.mean(table, axis=1, keepdims=True)
    table = center * lax.rsqrt(jnp.mean(center * center, axis=1, keepdims=True) + 1e-07)
    table = table.astype(bf16)
    tab_back = table[SPAN + ROW_LEN - 2 * ROW_LEN : SPAN + ROW_LEN][::-1]
    tab_on = table[SPAN - ROW_LEN + 1 : SPAN + ROW_LEN + 1]
    return layers, jnp.zeros((1,), jnp.int32), bias, factors, tab_back, tab_on, small


def spread_kernel(order_ref, *refs):
    keep_ref, send_ref, whole, cut = refs[3 * LAYERS :]
    half, _, rows, wide = keep_ref.shape
    cols = COLS // (2 * half)
    whole[:, COLS:] = jnp.zeros_like(whole[:, COLS:])
    lane = lax.broadcasted_iota(jnp.int32, (rows, wide), 1)
    for i in range(LAYERS):
        dpt_ref, dq_ref, dl_ref = refs[3 * i : 3 * i + 3]
        whole[:, :COLS] = jnp.concatenate([dpt_ref[:RANK], dq_ref[:RANK]], axis=0)
        dl = jnp.concatenate([dl_ref[:RANK, :6], jnp.zeros((rows - RANK, 6), f32)], axis=0)
        parts = [jnp.zeros((rows, cols), f32), dl, jnp.zeros((rows, wide - cols - 6), f32)]
        extra = jnp.concatenate(parts, axis=1)
        for p in range(2 * half):
            cut[p] = jnp.where(lane < cols, whole[:, p * cols : p * cols + wide], extra)

        def place_step(k, carry):
            keep_ref[k, i] = cut[order_ref[k]]
            send_ref[k, i] = cut[order_ref[half + k]].astype(bf16)
            return carry

        lax.fori_loop(0, half, place_step, 0)


def spread(order, grads, count):
    cols = COLS // count
    wide = 128 * (-(-(cols + 6) // 128))
    dims = (count // 2, LAYERS, 2 * RANK, wide)
    return pl.pallas_call(
        spread_kernel,
        out_shape=[shape(dims, f32), shape(dims, bf16)],
        in_specs=[SM] + [VM] * (3 * LAYERS),
        out_specs=[VM, VM],
        scratch_shapes=[
            pltpu.VMEM((2 * RANK, COLS + wide), f32),
            pltpu.VMEM((count, 2 * RANK, wide), f32),
        ],
        compiler_params=pltpu.CompilerParams(vmem_limit_bytes=LIMIT),
        name="spread",
    )(order, *[part for layer in grads for part in layer])


def reduce_grads(grads, count, place):
    bits = count.bit_length() - 1
    routes = [[(d, d ^ (1 << b)) for d in range(count)] for b in range(bits)]
    number = np.arange(count)
    picks = [(number >> (bits - 1 - s)) & 1 for s in range(bits)]
    steps = [np.full((count,), 1 << s) for s in range(bits)]
    if count == 32:
        routes[1], routes[2] = TO_FIRST, TO_OTHER
        swapped = flip(place % 2, picks[0])
        steps[1] = jnp.where(swapped == 0, 2, 4)
        steps[2] = 6 - steps[1]
    move = sum(pick * step for pick, step in zip(picks, steps))
    order = jnp.bitwise_xor(place, move.astype(jnp.int32))
    keep, away = spread(order, grads, count)
    if count == 32:
        keep = keep + send(away, routes[0])
        for places, last in ((4, (TO_FIRST, TO_OTHER, TO_DIAGONAL)), (1, (TO_Z1, TO_Z2, TO_Z3))):
            low = keep[places:].astype(bf16)
            got = [
                send(low[(at - 1) * places : at * places], route) for at, route in zip((2, 1, 3), last)
            ]
            keep = keep[:places] + got[0] + got[1] + got[2]
    else:
        for s in range(bits):
            got = send(away, routes[s])
            half = keep.shape[0] // 2
            if half:
                away = (keep[half:] + got[half:]).astype(bf16)
            keep = keep[: max(half, 1)] + got[: max(half, 1)]
    total = keep[0]
    cols = COLS // count
    factor_share = total[:, :, :cols].reshape(LAYERS, 2, RANK, cols)
    return factor_share, jnp.swapaxes(total[:, :RANK, cols : cols + 6], 1, 2)


def on_device(
    hidden_in,
    frozen_weights,
    adapter_factors,
    strengths,
    relative,
    segment_ids,
    row_lengths,
    cotangent,
):
    count = lax.axis_size(BOTH)
    place = lax.axis_index(BOTH)
    scales = jnp.pad(strengths, ((0, 0), (0, 2), (0, 128 - RANK)))
    scales_t = jnp.pad(
        jnp.swapaxes(strengths, 1, 2), ((0, 0), (0, RP - RANK), (0, 128 - 6))
    )
    live = jnp.arange(ROW_LEN, dtype=jnp.int32) < row_lengths[0]
    segc = jnp.where(live, segment_ids, -1).reshape(ROW_LEN, 1)
    segr = jnp.where(live, segment_ids, -2).reshape(1, ROW_LEN)
    gather = gather_all if count == 32 else gather_plain
    layers, places, bias, factors, tab_back, tab_on, small = gather(
        frozen_weights, adapter_factors, relative, count, place,
        [scales, scales_t, segc, segr, hidden_in.astype(f32)],
    )
    scales, scales_t, segc, segr, start = small

    flow = None if isinstance(layers, list) else layers
    states = [start]
    records = []
    if flow:
        layers = [flow.layer(0)]
        states[0] = flow.tie(states[0])
    for i in range(LAYERS):
        if flow and i == 1:
            flow.end(states[1])
            flow.run(flow.after)
            layers.append(flow.layer(1))
        y, *record = run_forward(
            states[-1], layers[i], places, bias[i], factors[i, 0], factors[i, 1], scales[i],
            tab_back, segc, segr,
        )
        states.append(y)
        records.append(record)
    grad = cotangent
    grads = [None] * LAYERS
    for i in reversed(range(LAYERS)):
        grad, *grads[i] = run_backward(
            grad, states[i], layers[i], places, bias[i], factors[i, 0], factors[i, 1], scales[i],
            scales_t[i], tab_on, records[i],
        )
    factor_share, scale_total = reduce_grads(grads, count, place)
    return states[-1], grad, factor_share, scale_total


def solution(mesh):
    in_specs = (
        P(BOTH, None),
        P(None, BOTH),
        P(None, None, None, BOTH),
        P(),
        P(BOTH),
        P(BOTH),
        P(BOTH),
        P(BOTH, None),
    )
    out_specs = (P(BOTH, None), P(BOTH, None), P(None, None, None, BOTH), P())
    return jax.shard_map(
        on_device, mesh=mesh, in_specs=in_specs, out_specs=out_specs, check_vma=False
    )
```
